32 devices in a mesh: group: 2 (over y), ctx: 8 (over z, core), head: 2 (over x).
Axes of the slice: x: 2, y: 2, z: 4, core: 2. Of those that a mesh axis runs over, the one named last changes fastest.
Arguments:
- queries: bfloat16 [2048, 4096], P(('group', 'ctx'), 'head'), parts along dimension 0, may hold values from -6 to 6
- keys: bfloat16 [2048, 512], P(('group', 'ctx'), 'head'), parts along dimension 0, may hold values from -6 to 6
- values: bfloat16 [2048, 512], P(('group', 'ctx'), 'head'), parts along dimension 0, may hold values from -6 to 6
- sinks: float32 [64], P('head'), may hold values from 0 to 4
- segments: int32 [2048], P('group'), parts along dimension 0, may hold values from 0 to 3, never falling along the last dimension, each value on 1 to 768 neighbouring positions
- hidden_in: bfloat16 [2048, 2880], P(('group', 'ctx')), parts along dimension 0, may hold values from -6 to 6
- routes: int32 [2048, 4], P(('group', 'ctx')), parts along dimension 0, may hold values from 0 to 7, all different within a row; in each aligned block of 64 rows (0 to 63, 64 to 127, ...) at most 48 rows name the same one
- w_out: bfloat16 [4096, 2880], P('head'), may hold values from -0.09375 to 0.09375
- norm_gain: float32 [2880], replicated, may hold values from 0.1 to 1.9
- router: bfloat16 [2880, 8], replicated, may hold values from -0.109375 to 0.109375
- w_gate_up: bfloat16 [8, 2, 2880, 2880], P('ctx', None, None, 'head'), may hold values from -0.109375 to 0.109375
- w_down: bfloat16 [8, 2880, 2880], P('ctx', 'head'), may hold values from -0.109375 to 0.109375
Outputs:
- layer_out: bfloat16 [2048, 2880], P(('group', 'ctx', 'head')), parts along dimension 0
The draws below stay inside these ranges and needn't reach their ends.
There are 2 independent parts, one for each index of `group`. The reference program is written for one: setup_inputs(seed, part) draws one part's arguments, and reference() takes and returns one part's arrays. A program takes and returns all parts, laid end to end along the dimension named above; an argument that names none is the same for every part. Nothing has to cross between parts.
Inputs may be any that keep to these rules, and one draw needn't show every extreme that they name: `routes`: each row names 4 different experts; in each aligned block of 64 rows no expert is named by more than 48 rows, a bound that some block reaches. `segments`: requests fill consecutive positions in order; the longest has 768 positions.
All inputs are finite; a program needn't handle non-finite values.
Results may differ from the reference program's by a relative error of at most 0.015.
Values may be sent and summed in bfloat16 or wider, within the bound.
A program may use at most 128 MiB of HBM per device.

```python
import math
import jax
import jax.numpy as jnp
import numpy as np
from jax import lax

D = 2880
QUERY_HEADS = 64
KEY_VALUE_HEADS = 8
HEAD_SIZE = 64
FF = 2880
TOPK = 4
TOTAL_POSITIONS = 1024
EXPERTS = 8
ROWS_DEV = 64
CAP = 48
SLICE = 1440
N_CTX = 8
N_HEAD = 2


def query_key_pair(key):
    first, second_choice = jax.random.split(key, 2)
    queries = jnp.clip(jax.random.normal(first, (TOTAL_POSITIONS, QUERY_HEADS * HEAD_SIZE), jnp.float32), -6.0, 6.0)
    keys = jnp.clip(jax.random.normal(second_choice, (TOTAL_POSITIONS, KEY_VALUE_HEADS * HEAD_SIZE), jnp.float32), -6.0, 6.0)
    return (queries, keys)


def draw_queries(key, part):
    return query_key_pair(key)[0].astype(jnp.bfloat16)


def draw_keys(key, part):
    return query_key_pair(key)[1].astype(jnp.bfloat16)


def shard_levels(own_key, shape, cuts, smallest, top_value):
    def one(dim, blocks):
        steps = jax.random.uniform(jax.random.fold_in(jax.random.fold_in(own_key, 6), dim), (blocks,), jnp.float32, smallest / len(cuts), top_value / len(cuts))
        return jnp.repeat(jnp.exp(steps), shape[dim] // blocks).reshape((-1,) + (1,) * (len(shape) - dim - 1))

    loudness = one(*cuts[0])
    for cut in cuts[1:]:
        loudness = loudness * one(*cut)
    return loudness


def split_up(count, total, reach, skew):
    portions = [(1 << 20) // math.isqrt(rank ** skew) + 1 for rank in range(2, count + 1)]
    surplus, holding = total - reach - (count - 1), [1] * (count - 1)
    while surplus > 0:
        free = [i for i in range(count - 1) if holding[i] < reach]
        whole, left = sum([portions[i] for i in free]), surplus
        for i in free:
            addition = min(reach - holding[i], max(1, left * portions[i] // whole), surplus)
            holding[i] = holding[i] + addition
            surplus = surplus - addition
    return np.array([reach] + holding)


def uneven_parts(stream_key, count, total, bound, skew):
    if count == 2:
        one = jax.random.randint(stream_key, (), max(1, total - bound), min(bound, total - 1) + 1)
        return jnp.stack([one, total - one])
    tallies = jnp.asarray(split_up(count, total, bound, skew), jnp.int32)
    twos = (count - 1) // 2
    donor, taker = tallies[1:1 + 2 * twos:2], tallies[2:2 + 2 * twos:2]
    margin = jnp.minimum(donor - 1, bound - taker)
    passed = jax.random.randint(jax.random.fold_in(stream_key, 1), (twos,), 0, 1 << 20) % (margin + 1)
    tallies = tallies.at[1:1 + 2 * twos:2].set(donor - passed).at[2:2 + 2 * twos:2].set(taker + passed)
    return tallies[jax.random.permutation(jax.random.fold_in(stream_key, 2), count)]


def deal_out(stream_key, own, number, rows, amount, top, limit, lean):
    ranking = jax.random.permutation(stream_key, amount)
    heavy_load, usual = load_shares(amount, rows * top, limit, lean, True), load_shares(amount, rows * top, limit, lean, False)
    places = jnp.arange(amount)

    def named(tallies, offset_by):
        used = int((tallies > 0).sum())
        fixed = max(1, used // 4)
        shifted = fixed + (places - fixed + offset_by * (used - fixed)) % max(1, amount - fixed)
        return jnp.zeros((amount,), jnp.int32).at[ranking[jnp.where(places < fixed, places, shifted)]].set(jnp.asarray(tallies, jnp.int32))

    tallies = jnp.where(number % 4 == 0, named(heavy_load, number // 4), named(usual, number - number // 4 - 1))
    mixed = jax.random.permutation(jax.random.fold_in(own, 3), amount)
    source_of, receiver = mixed[0:amount // 2 * 2:2], mixed[1:amount // 2 * 2:2]
    slack = jnp.minimum(tallies[source_of] - 1, limit - tallies[receiver]) // 2
    slack = jnp.where((source_of == ranking[0]) | (receiver == ranking[0]) | (tallies[receiver] == 0), 0, jnp.maximum(slack, 0))
    shifted = jax.random.randint(jax.random.fold_in(own, 4), (amount // 2,), 0, 1 << 20) % (slack + 1)
    tallies = tallies.at[source_of].add(-shifted).at[receiver].add(shifted)
    labels = jnp.searchsorted(jnp.cumsum(tallies), jnp.arange(rows * top), side="right").astype(jnp.int32)
    table = labels.reshape(top, rows).T
    table = table[jax.random.permutation(jax.random.fold_in(own, 1), rows)]
    offset_by = jax.random.randint(jax.random.fold_in(own, 2), (rows, 1), 0, top)
    return jnp.take_along_axis(table, (jnp.arange(top)[None, :] + offset_by) % top, axis=1)


def load_shares(amount, total, most, skew, full):
    portions = [(1 << 20) // math.isqrt(grade ** skew) + 1 for grade in range(1, amount + 1)]
    largest = most if full else min(most, max(-(-total // amount), total * portions[0] // sum(portions)))
    least = 1 if total - largest >= amount - 1 else 0
    counts, rest = [largest] + [least] * (amount - 1), total - largest - least * (amount - 1)
    while rest > 0:
        candidates = [i for i in range(1, amount) if counts[i] < largest] or [i for i in range(1, amount) if counts[i] < most]
        whole, remaining = sum([portions[i] for i in candidates]), rest
        for i in candidates:
            addition = min(most - counts[i], max(1, remaining * portions[i] // whole), rest)
            counts[i] = counts[i] + addition
            rest = rest - addition
    return np.array(counts)


def bell_draw(rng, extent, width, most, cuts=(), kind=jnp.bfloat16):
    values = jax.random.normal(rng, extent, jnp.float32) * width
    if len(cuts) > 0:
        values = shard_levels(rng, extent, cuts, -0.22, 0.18) * values
    return jnp.clip(values, min=-most, max=most).astype(kind)


def setup_inputs(seed: int = 0, part: int = 0) -> dict:
    key_of = jax.random.split(jax.random.key(seed), 13)
    part_keys = jax.random.split(jax.random.fold_in(key_of[12], part), 13)
    queries = draw_queries(jax.random.fold_in(jax.random.fold_in(key_of[12], part), 71), part)
    keys = draw_keys(jax.random.fold_in(jax.random.fold_in(key_of[12], part), 71), part)
    values = bell_draw(part_keys[2], (TOTAL_POSITIONS, KEY_VALUE_HEADS * HEAD_SIZE), 1.0, 6.0, ((0, 8), (1, 2)))
    sinks = jnp.clip(4.0 * jax.random.uniform(key_of[3], (QUERY_HEADS,), jnp.float32) ** shard_levels(key_of[3], (QUERY_HEADS,), ((0, 2),), -0.2, 0.2), 0.0, 4.0)
    segments = jnp.searchsorted(jnp.cumsum(uneven_parts(part_keys[4], 4, TOTAL_POSITIONS, 3 * TOTAL_POSITIONS // 4, 0)), jnp.arange(TOTAL_POSITIONS), side="right").astype(jnp.int32)
    hidden_in = bell_draw(part_keys[5], (TOTAL_POSITIONS, D), 1.0, 6.0, ((0, 8),))
    routes_keys = jax.random.split(jax.random.fold_in(part_keys[6], 1), TOTAL_POSITIONS // ROWS_DEV)
    routes_turns = jax.random.permutation(jax.random.fold_in(part_keys[6], 3), TOTAL_POSITIONS // ROWS_DEV)
    routes = jax.vmap(lambda own, number: deal_out(jax.random.fold_in(part_keys[6], 2), own, number, ROWS_DEV, EXPERTS, TOPK, CAP, 2))(routes_keys, routes_turns).reshape((TOTAL_POSITIONS, TOPK))
    w_out = bell_draw(key_of[7], (QUERY_HEADS * HEAD_SIZE, D), (QUERY_HEADS * HEAD_SIZE) ** -0.5, 0.09375, ((0, 2),))
    norm_gain = jnp.clip(1.0 + 0.18 * jax.random.normal(key_of[8], (D,), jnp.float32), 0.1, 1.9)
    router = bell_draw(key_of[9], (D, EXPERTS), D ** -0.5, 0.109375)
    w_gate_up = bell_draw(key_of[10], (EXPERTS, 2, D, FF), D ** -0.5, 0.109375, ((0, 8), (3, 2)))
    w_down = bell_draw(key_of[11], (EXPERTS, FF, D), FF ** -0.5, 0.109375, ((0, 8), (1, 2)))
    return {"queries": queries, "keys": keys, "values": values, "sinks": sinks, "segments": segments, "hidden_in": hidden_in, "routes": routes, "w_out": w_out, "norm_gain": norm_gain, "router": router, "w_gate_up": w_gate_up, "w_down": w_down}


masked_value = -1e+30

def reference(queries, keys, values, sinks, segments, hidden_in, routes, w_out, norm_gain, router, w_gate_up, w_down):
    group_share = QUERY_HEADS // KEY_VALUE_HEADS
    positions = jnp.arange(TOTAL_POSITIONS, dtype=jnp.int32)
    visible = (positions[None, :] <= positions[:, None]) & (segments[None, :] == segments[:, None])

    def key_value_share(kv_index):
        query_part = lax.dynamic_slice_in_dim(queries, kv_index * group_share * HEAD_SIZE, group_share * HEAD_SIZE, 1)
        query_part = query_part.reshape(TOTAL_POSITIONS, group_share, HEAD_SIZE).astype(jnp.float32)
        key_part = lax.dynamic_slice_in_dim(keys, kv_index * HEAD_SIZE, HEAD_SIZE, 1).astype(jnp.float32)
        value_part = lax.dynamic_slice_in_dim(values, kv_index * HEAD_SIZE, HEAD_SIZE, 1).astype(jnp.float32)
        sink_part = lax.dynamic_slice_in_dim(sinks, kv_index * group_share, group_share, 0)
        scores = jnp.einsum('tgd,nd->gtn', query_part, key_part) * HEAD_SIZE ** (-0.5)
        scores = jnp.where(visible[None], scores, masked_value)
        top_score = jnp.maximum(sink_part[:, None], lax.optimization_barrier(jnp.max(scores, axis=-1)))
        probs = jnp.where(visible[None], jnp.exp(scores - top_score[..., None]), 0.0)
        denom = lax.optimization_barrier(jnp.sum(probs, axis=-1)) + jnp.exp(sink_part[:, None] - top_score)
        probs_b = lax.optimization_barrier(probs.astype(jnp.bfloat16)).astype(jnp.float32)
        attended = jnp.einsum('gtn,nd->gtd', probs_b, value_part) / denom[..., None]
        return attended.astype(jnp.bfloat16).transpose(1, 0, 2)
    head_share = lax.map(key_value_share, jnp.arange(KEY_VALUE_HEADS, dtype=jnp.int32))
    attended = head_share.transpose(1, 0, 2, 3).reshape(TOTAL_POSITIONS, QUERY_HEADS * HEAD_SIZE)
    projected = jnp.dot(attended, w_out, preferred_element_type=jnp.float32)
    residual = (hidden_in.astype(jnp.float32) + projected).astype(jnp.bfloat16)
    widened = residual.astype(jnp.float32)
    normed = (widened * lax.rsqrt(lax.optimization_barrier(jnp.mean(widened * widened, axis=-1, keepdims=True)) + 1e-05) * norm_gain).astype(jnp.bfloat16)
    logits = jnp.dot(normed, router, preferred_element_type=jnp.float32)
    gates = jax.nn.softmax(jnp.take_along_axis(logits, routes, axis=1), axis=-1)
    rows_max = min(TOTAL_POSITIONS, N_CTX * N_HEAD * CAP)
    token_index = jnp.arange(TOTAL_POSITIONS, dtype=jnp.int32)

    def per_expert(carried, expert):
        chosen = routes == expert
        selected = jnp.any(chosen, axis=1)
        weight = lax.optimization_barrier(jnp.sum(jnp.where(chosen, gates, 0.0), axis=1))
        order_key = jnp.where(selected, token_index, TOTAL_POSITIONS + token_index)
        taken = jnp.argsort(order_key)[:rows_max].astype(jnp.int32)
        token_rows = normed[taken]
        gate_up = lax.dynamic_index_in_dim(w_gate_up, expert, 0, keepdims=False)
        down_full = lax.dynamic_index_in_dim(w_down, expert, 0, keepdims=False)
        gate_pre = jnp.dot(token_rows, gate_up[0], preferred_element_type=jnp.float32)
        up_pre = jnp.dot(token_rows, gate_up[1], preferred_element_type=jnp.float32)
        activation = (gate_pre * jax.nn.sigmoid(1.702 * gate_pre) * (up_pre + 1.0)).astype(jnp.bfloat16)
        act_slices = activation.reshape(rows_max, N_HEAD, SLICE).astype(jnp.float32)
        down_slices = down_full.reshape(N_HEAD, SLICE, D).astype(jnp.float32)
        pieces = jnp.einsum('msf,sfd->smd', act_slices, down_slices).astype(jnp.bfloat16)
        pieces = lax.optimization_barrier(pieces)
        expert_out = lax.optimization_barrier(jnp.sum(pieces.astype(jnp.float32), axis=0)).astype(jnp.bfloat16)
        contrib = weight[taken][:, None] * expert_out.astype(jnp.float32)
        return (carried.at[taken].add(contrib), None)
    mixture, _ = lax.scan(per_expert, jnp.zeros((TOTAL_POSITIONS, D), jnp.float32), jnp.arange(EXPERTS, dtype=jnp.int32))
    return (residual.astype(jnp.float32) + mixture).astype(jnp.bfloat16)
```

```python
import jax
import jax.numpy as jnp
from jax import lax
from jax.sharding import PartitionSpec as P

HEAD_SIZE = 64


masked_value = -1e30


def fold_step(state_in, pieces, query_grid, tok_pos, tok_seg, segments):
    running_max, running_sum, weighted = state_in
    key_piece, value_piece = pieces
    row_count = key_piece.shape[0]
    kv_groups = query_grid.shape[1]
    key_grid = key_piece.reshape(row_count, kv_groups, -1)
    value_grid = value_piece.reshape(row_count, kv_groups, -1)
    scores = jnp.einsum(
        "tcgd,ncd->cgtn", query_grid, key_grid, preferred_element_type=jnp.float32
    ) * HEAD_SIZE ** (-0.5)
    key_pos = jnp.arange(row_count, dtype=jnp.int32)
    visible = (key_pos[None, :] <= tok_pos[:, None]) & (segments[None, :] == tok_seg[:, None])
    scores = jnp.where(visible, scores, masked_value)
    new_max = jnp.maximum(running_max, jnp.max(scores, axis=-1))
    weights = jnp.where(visible, jnp.exp(scores - new_max[..., None]), 0.0)
    rescale = jnp.exp(running_max - new_max)
    running_sum = running_sum * rescale + jnp.sum(weights, axis=-1)
    weighted = weighted * rescale[..., None] + jnp.einsum(
        "cgtn,ncd->cgtd",
        weights.astype(jnp.bfloat16),
        value_grid,
        preferred_element_type=jnp.float32,
    )
    return (new_max, running_sum, weighted)


def rms_norm(residual, norm_gain):
    widened = residual.astype(jnp.float32)
    scale_rows = lax.rsqrt(jnp.mean(widened * widened, axis=-1, keepdims=True) + 1e-05)
    return (widened * scale_rows * norm_gain).astype(jnp.bfloat16)


def expert_gates(normed_rows, router, route_rows, expert):
    logits = jnp.dot(normed_rows, router, preferred_element_type=jnp.float32)
    onehot = (
        route_rows[:, :, None] == jnp.arange(router.shape[1], dtype=jnp.int32)[None, None, :]
    ).astype(jnp.float32)
    picked = jnp.sum(onehot * logits[:, None, :], axis=-1)
    gates = jax.nn.softmax(picked, axis=-1)
    return jnp.sum(jnp.where(route_rows == expert, gates, 0.0), axis=1)


def expert_activation(token_rows, w_gate_up):
    gate_pre = jnp.dot(token_rows, w_gate_up[0, 0], preferred_element_type=jnp.float32)
    up_pre = jnp.dot(token_rows, w_gate_up[0, 1], preferred_element_type=jnp.float32)
    return (gate_pre * jax.nn.sigmoid(1.702 * gate_pre) * (up_pre + 1.0)).astype(jnp.bfloat16)


def body(
    queries,
    keys,
    values,
    sinks,
    segments,
    hidden_in,
    routes,
    w_out,
    norm_gain,
    router,
    w_gate_up,
    w_down,
):
    n_ctx = lax.axis_size("ctx")
    n_head = lax.axis_size("head")
    tok_count = queries.shape[0]
    top_count = routes.shape[1]
    kv_groups = keys.shape[1] // HEAD_SIZE
    group_share = queries.shape[1] // (kv_groups * HEAD_SIZE)
    q_start = lax.axis_index("ctx") * tok_count
    tok_pos = q_start + jnp.arange(tok_count, dtype=jnp.int32)
    tok_seg = lax.dynamic_slice_in_dim(segments, q_start, tok_count, 0)
    query_grid = queries.reshape(tok_count, kv_groups, group_share, HEAD_SIZE)
    sink_grid = sinks.reshape(kv_groups, group_share, 1) * jnp.ones((1, 1, tok_count), jnp.float32)
    initial = (
        sink_grid,
        jnp.ones_like(sink_grid),
        jnp.zeros((kv_groups, group_share, tok_count, HEAD_SIZE), jnp.float32),
    )
    kv_width = keys.shape[1]
    packed = jnp.concatenate(
        [keys, values, jnp.pad(routes.astype(jnp.bfloat16), ((0, 0), (0, 128 - top_count)))], axis=1
    )
    gathered = lax.all_gather(packed, "ctx", axis=0, tiled=True)
    all_routes = gathered[:, 2 * kv_width : 2 * kv_width + top_count].astype(jnp.int32)
    running_max, running_sum, weighted = fold_step(
        initial,
        (gathered[:, :kv_width], gathered[:, kv_width : 2 * kv_width]),
        query_grid,
        tok_pos,
        tok_seg,
        segments,
    )
    attended = (
        (weighted / running_sum[..., None])
        .transpose(2, 0, 1, 3)
        .reshape(tok_count, -1)
        .astype(jnp.bfloat16)
    )
    own_rows = tok_count // n_head
    row_start = lax.axis_index("head") * own_rows
    capacity = max(2, min(tok_count // n_head, 3 * tok_count * top_count // (2 * n_head * n_ctx)))
    head_sums = lax.psum_scatter(
        jnp.dot(attended, w_out, preferred_element_type=jnp.float32).astype(jnp.bfloat16),
        "head",
        scatter_dimension=0,
        tiled=True,
    ).astype(jnp.float32)
    own_hidden = lax.dynamic_slice_in_dim(hidden_in, row_start, own_rows, 0)
    residual = (own_hidden.astype(jnp.float32) + head_sums).astype(jnp.bfloat16)
    normed = rms_norm(residual, norm_gain)
    expert = lax.axis_index("ctx")
    blocks = n_ctx * n_head
    normed_all = lax.all_gather(normed, ("ctx", "head"), axis=0, tiled=True)
    gate = expert_gates(normed_all, router, all_routes, expert).reshape(blocks, own_rows)
    chosen = jnp.any(all_routes == expert, axis=1).reshape(blocks, own_rows)
    rank = jnp.cumsum(chosen.astype(jnp.int32), axis=1) - 1
    place = (
        (rank[:, None, :] == jnp.arange(capacity, dtype=jnp.int32)[None, :, None])
        & chosen[:, None, :]
    )
    token_rows = jnp.einsum(
        "bcr,brd->bcd",
        place.astype(jnp.bfloat16),
        normed_all.reshape(blocks, own_rows, -1),
        preferred_element_type=jnp.float32,
    ).astype(jnp.bfloat16)
    row_gate = jnp.sum(jnp.where(place, gate[:, None, :], 0.0), axis=2).reshape(-1, 1)
    activation = expert_activation(token_rows.reshape(blocks * capacity, -1), w_gate_up)
    pieces = jnp.dot(activation, w_down[0], preferred_element_type=jnp.float32)
    gated = (pieces * row_gate).astype(jnp.bfloat16).reshape(blocks, capacity, -1)
    spread = jnp.einsum(
        "bcr,bcd->brd", place.astype(jnp.bfloat16), gated, preferred_element_type=jnp.float32
    ).astype(jnp.bfloat16)
    mixed = lax.psum_scatter(
        spread.reshape(blocks * own_rows, -1), ("ctx", "head"), scatter_dimension=0, tiled=True
    )
    return (residual.astype(jnp.float32) + mixed.astype(jnp.float32)).astype(jnp.bfloat16)


def solution(mesh):
    placed = (
        P(("group", "ctx"), "head"),
        P(("group", "ctx"), "head"),
        P(("group", "ctx"), "head"),
        P("head"),
        P("group"),
        P(("group", "ctx"), None),
        P(("group", "ctx"), None),
        P("head", None),
        P(),
        P(),
        P("ctx", None, None, "head"),
        P("ctx", "head", None),
    )
    return jax.shard_map(
        body,
        mesh=mesh,
        in_specs=placed,
        out_specs=P(("group", "ctx", "head"), None),
        check_vma=False,
    )
```

```python
import functools

import jax
import jax.numpy as jnp
from jax import lax
from jax.experimental import pallas as pl
from jax.experimental.pallas import tpu as pltpu
from jax.sharding import PartitionSpec as P

HEAD_SIZE = 64


masked_value = -1e30


def fold_step(state_in, pieces, query_grid, tok_pos, tok_seg, segments):
    running_max, running_sum, weighted = state_in
    key_piece, value_piece = pieces
    row_count = key_piece.shape[0]
    kv_groups = query_grid.shape[1]
    key_grid = key_piece.reshape(row_count, kv_groups, -1)
    value_grid = value_piece.reshape(row_count, kv_groups, -1)
    scores = jnp.einsum(
        "tcgd,ncd->cgtn", query_grid, key_grid, preferred_element_type=jnp.float32
    ) * HEAD_SIZE ** (-0.5)
    key_pos = jnp.arange(row_count, dtype=jnp.int32)
    visible = (key_pos[None, :] <= tok_pos[:, None]) & (segments[None, :] == tok_seg[:, None])
    scores = jnp.where(visible, scores, masked_value)
    new_max = jnp.maximum(running_max, jnp.max(scores, axis=-1))
    weights = jnp.where(visible, jnp.exp(scores - new_max[..., None]), 0.0)
    rescale = jnp.exp(running_max - new_max)
    running_sum = running_sum * rescale + jnp.sum(weights, axis=-1)
    weighted = weighted * rescale[..., None] + jnp.einsum(
        "cgtn,ncd->cgtd",
        weights.astype(jnp.bfloat16),
        value_grid,
        preferred_element_type=jnp.float32,
    )
    return (new_max, running_sum, weighted)


MESH = pl.DeviceIdType.MESH
LANES = 128
CORES = 2


def full_vmem():
    return pl.BlockSpec(memory_space=pltpu.VMEM)


class Ring:
    def __init__(self, chips, heads):
        self.chips, self.heads, self.count = chips, heads, chips * heads
        ctx = lax.axis_index("ctx")
        self.head = lax.axis_index("head")
        self.core = lax.rem(ctx, CORES)
        z = lax.div(ctx, CORES)
        self.place = self.head * chips + z + lax.rem(self.head, 2) * (chips - 1 - 2 * z)
        self.partner = {"ctx": z * CORES + 1 - self.core, "head": self.head}

    def at(self, offset):
        spot = lax.rem(self.place + offset + self.count, self.count)
        head = lax.div(spot, self.chips)
        step = lax.rem(spot, self.chips)
        return head, step + lax.rem(head, 2) * (self.chips - 1 - 2 * step)

    def block(self, offset, core):
        head, z = self.at(offset)
        return (z * CORES + core) * self.heads + head

    def device(self, offset):
        head, z = self.at(offset)
        return {"ctx": z * CORES + self.core, "head": head}


def remote(src, dst, send_sem, recv_sem, device):
    return pltpu.make_async_remote_copy(
        src_ref=src, dst_ref=dst, send_sem=send_sem, recv_sem=recv_sem, device_id=device, device_id_type=MESH
    )


def greet(devices):
    barrier = pltpu.get_barrier_semaphore()
    for device in devices:
        pl.semaphore_signal(barrier, inc=1, device_id=device, device_id_type=MESH)
    pl.semaphore_wait(barrier, len(devices))


def row_chunks(rows):
    if rows % 32 == 0:
        return [pl.ds(0, rows // 2), pl.ds(rows // 2, rows // 2)]
    return [pl.ds(0, rows)]


def line_kernel(chips, key_ref, value_ref, all_keys, all_values, line_send, line_recv, pair_send, pair_recv, own_sem):
    ctx = lax.axis_index("ctx")
    z, core = lax.div(ctx, CORES), lax.rem(ctx, CORES)
    ins, outs = (key_ref, value_ref), (all_keys, all_values)
    partner = {"ctx": z * CORES + 1 - core}
    ways = ((0, 1), (1, -1))

    def inside(spot):
        return (spot >= 0) & (spot < chips)

    barrier = pltpu.get_barrier_semaphore()
    pl.semaphore_signal(barrier, inc=1, device_id=partner, device_id_type=MESH)
    for _, way in ways:

        @pl.when(inside(z + way))
        def _():
            pl.semaphore_signal(
                barrier, inc=1, device_id={"ctx": (z + way) * CORES + core}, device_id_type=MESH
            )

    peers = 1 + sum(jnp.where(inside(z + way), 1, 0) for _, way in ways)
    pl.semaphore_wait(barrier, peers)

    def hop(index, way, step, part):
        block = (z - way * step) * CORES + core
        source = ins[part] if step == 0 else outs[part].at[block]
        return remote(
            source,
            outs[part].at[block],
            line_send.at[index, step, part],
            line_recv.at[index, step, part],
            {"ctx": (z + way) * CORES + core},
        )

    def share(slot, block, part):
        source = ins[part] if slot == 0 else outs[part].at[block]
        return remote(source, outs[part].at[block], pair_send.at[slot, part], pair_recv.at[slot, part], partner)

    def keep(part):
        return pltpu.make_async_copy(ins[part], outs[part].at[ctx], own_sem.at[part])

    for part in (0, 1):
        for index, way in ways:

            @pl.when(inside(z + way))
            def _():
                hop(index, way, 0, part).start()

    for part in (0, 1):
        share(0, ctx, part).start()
        keep(part).start()
    for step in range(1, chips):
        for part in (0, 1):
            for index, way in ways:

                @pl.when(inside(z - way * step))
                def _():
                    hop(index, way, step - 1, part).wait_recv()
                    if step < chips - 1:

                        @pl.when(inside(z + way))
                        def _():
                            hop(index, way, step, part).start()

                    share(index * (chips - 1) + step, (z - way * step) * CORES + core, part).start()

    for part in (0, 1):
        keep(part).wait()
        share(0, ctx, part).wait()
        for index, way in ways:
            for step in range(chips):
                if step < chips - 1:

                    @pl.when(inside(z + way) & inside(z - way * step))
                    def _():
                        hop(index, way, step, part).wait_send()

                if step > 0:

                    @pl.when(inside(z - way * step))
                    def _():
                        share(index * (chips - 1) + step, (z - way * step) * CORES + core, part).wait()


def gather_keys(keys, values):
    n_ctx = lax.axis_size("ctx")
    chips = n_ctx // CORES
    shape = jax.ShapeDtypeStruct((n_ctx,) + keys.shape, keys.dtype)
    slots = 2 * (chips - 1) + 1
    gathered = pl.pallas_call(
        functools.partial(line_kernel, chips),
        out_shape=(shape, shape),
        in_specs=[full_vmem()] * 2,
        out_specs=(full_vmem(),) * 2,
        scratch_shapes=[
            pltpu.SemaphoreType.DMA((2, chips, 2)),
            pltpu.SemaphoreType.DMA((2, chips, 2)),
            pltpu.SemaphoreType.DMA((slots, 2)),
            pltpu.SemaphoreType.DMA((slots, 2)),
            pltpu.SemaphoreType.DMA((2,)),
        ],
        compiler_params=pltpu.CompilerParams(collective_id=0, has_side_effects=True),
        name="gather_keys",
    )(keys, values)
    return [array.reshape(-1, array.shape[-1]) for array in gathered]


def norm_kernel(
    chips, heads, experts, part_ref, hidden_ref, gain_ref, router_ref, route_ref, residual_ref, all_ref,
    slots, head_send, head_recv, ring_send, ring_recv, pair_send, pair_recv,
):
    ring = Ring(chips, heads)
    count, half = ring.count, ring.count // 2
    rows, width = hidden_ref.shape
    ctx, head = lax.axis_index("ctx"), ring.head
    others = [{"ctx": ctx, "head": lax.rem(head + turn, heads)} for turn in range(1, heads)]
    greet([ring.device(1), ring.device(-1), ring.partner] + others)

    sends = []
    for turn, device in enumerate(others):
        target = pl.ds(pl.multiple_of(device["head"] * rows, rows), rows)
        copy = remote(part_ref.at[target], slots.at[turn], head_send.at[turn], head_recv.at[turn], device)
        copy.start()
        sends.append(copy)
    own = pl.ds(pl.multiple_of(head * rows, rows), rows)
    total = hidden_ref[...].astype(jnp.float32) + part_ref[own, :].astype(jnp.float32)
    for turn, copy in enumerate(sends):
        copy.wait_recv()
        total = total + slots[turn].astype(jnp.float32)
    residual = total.astype(jnp.bfloat16)
    residual_ref[...] = residual
    wide = residual.astype(jnp.float32)
    scale = lax.rsqrt(jnp.mean(wide * wide, axis=-1, keepdims=True) + 1e-05)
    normed = (wide * scale * gain_ref[...]).astype(jnp.bfloat16)

    logits = lax.dot_general(
        normed, router_ref[...], (((1,), (1,)), ((), ())), preferred_element_type=jnp.float32
    )
    start = width % LANES
    lane = lax.broadcasted_iota(jnp.int32, logits.shape, 1) - start
    first = (lane >= 0) & (lane < experts)
    present = jnp.zeros(logits.shape, jnp.bool_)
    for k in range(route_ref.shape[1]):
        route = route_ref[:, k : k + 1]
        present = present | (lane == route) | (lane - experts == route)
    top = jnp.max(jnp.where(present, logits, -jnp.inf), axis=-1, keepdims=True)
    powers = jnp.where(present, jnp.exp(jnp.where(present, logits - top, 0.0)), 0.0)
    gates = powers / jnp.sum(jnp.where(first, powers, 0.0), axis=-1, keepdims=True)
    coarse = gates.astype(jnp.bfloat16)
    rest = gates - coarse.astype(jnp.float32)
    mine = ring.block(0, ring.core)
    all_ref[mine, :, width - start :] = jnp.where(first, coarse.astype(jnp.float32), rest).astype(jnp.bfloat16)
    all_ref[mine, :, :width] = normed

    chunks = row_chunks(rows)
    hops, shares = {}, []

    def share(slot, block, j):
        view = all_ref.at[block, chunks[j]]
        copy = remote(view, view, pair_send.at[slot, j], pair_recv.at[slot, j], ring.partner)
        copy.start()
        shares.append(copy)

    for step in range(half + 1):
        for j in range(len(chunks)):
            for index, way in ((0, 1), (1, -1)):
                block = ring.block(-way * step, ring.core)
                if step > 0 and (index, step - 1, j) in hops:
                    hops[index, step - 1, j].wait_recv()
                if step < half - 1 or (step == half - 1 and (j == 0) == (index == 0)):
                    view = all_ref.at[block, chunks[j]]
                    hops[index, step, j] = remote(
                        view, view, ring_send.at[index, step, j], ring_recv.at[index, step, j], ring.device(way)
                    )
                    hops[index, step, j].start()
                if step == 0 and index == 0:
                    share(0, block, j)
                elif step > 0 and (index, step - 1, j) in hops:
                    share(index * half + step, block, j)
    for copy in sends + list(hops.values()):
        copy.wait_send()
    for copy in shares:
        copy.wait()


def norm_and_gather(partial_sums, own_hidden, norm_gain, router, own_routes):
    chips, heads = lax.axis_size("ctx") // CORES, lax.axis_size("head")
    rows, width = own_hidden.shape
    experts = router.shape[1]
    start = width % LANES
    padded = width - start + LANES
    half = chips * heads // 2
    parts = len(row_chunks(rows))
    turned = router.T
    lanes = jnp.concatenate(
        [
            jnp.zeros((start, width), router.dtype),
            turned,
            turned,
            jnp.zeros((LANES - start - 2 * experts, width), router.dtype),
        ],
        axis=0,
    )
    return pl.pallas_call(
        functools.partial(norm_kernel, chips, heads, experts),
        out_shape=(
            jax.ShapeDtypeStruct((rows, width), jnp.bfloat16),
            jax.ShapeDtypeStruct((chips * heads * CORES, rows, padded), jnp.bfloat16),
        ),
        in_specs=[full_vmem()] * 5,
        out_specs=(full_vmem(),) * 2,
        scratch_shapes=[
            pltpu.VMEM((heads - 1, rows, width), jnp.bfloat16),
            pltpu.SemaphoreType.DMA((heads - 1,)),
            pltpu.SemaphoreType.DMA((heads - 1,)),
            pltpu.SemaphoreType.DMA((2, half, parts)),
            pltpu.SemaphoreType.DMA((2, half, parts)),
            pltpu.SemaphoreType.DMA((2 * half + 1, parts)),
            pltpu.SemaphoreType.DMA((2 * half + 1, parts)),
        ],
        compiler_params=pltpu.CompilerParams(collective_id=1, has_side_effects=True),
        name="norm_and_gather",
    )(partial_sums, own_hidden, norm_gain.reshape(1, -1), lanes, own_routes)


def sum_kernel(
    chips, heads, term_ref, residual_ref, out_ref,
    got, outgoing, incoming, pair_send, pair_recv, ring_send, ring_recv,
):
    ring = Ring(chips, heads)
    half = ring.count // 2
    chunks = row_chunks(residual_ref.shape[0])
    greet([ring.device(1), ring.device(-1), ring.partner])
    order = [half]
    for distance in range(half - 1, 0, -1):
        order += [distance, -distance]
    order.append(0)
    shares = {}
    for slot, offset in enumerate(order):
        shares[offset] = remote(
            term_ref.at[ring.block(offset, 1 - ring.core)],
            got.at[slot],
            pair_send.at[slot],
            pair_recv.at[slot],
            ring.partner,
        )
        shares[offset].start()
    arrived = set()

    def pair(offset, chunk):
        if offset == -half:
            offset = half
        if offset not in arrived:
            shares[offset].wait_recv()
            arrived.add(offset)
        mine = term_ref[ring.block(offset, ring.core), chunk, :].astype(jnp.float32)
        return mine + got[order.index(offset), chunk, :].astype(jnp.float32)

    hops = {}
    for step in range(half):
        for j, chunk in enumerate(chunks):
            for index, way in ((0, 1), (1, -1)):
                if step == 0 and (j == 0) != (index == 0):
                    continue
                total = pair(way * (half - step), chunk)
                if (index, step - 1, j) in hops:
                    hops[index, step - 1, j].wait_recv()
                    total = total + incoming[index, step - 1, chunk, :].astype(jnp.float32)
                outgoing[index, step, chunk, :] = total.astype(jnp.bfloat16)
                hops[index, step, j] = remote(
                    outgoing.at[index, step, chunk],
                    incoming.at[index, step, chunk],
                    ring_send.at[index, step, j],
                    ring_recv.at[index, step, j],
                    ring.device(way),
                )
                hops[index, step, j].start()
    for j, chunk in enumerate(chunks):
        total = pair(0, chunk) + residual_ref[chunk, :].astype(jnp.float32)
        for index in (0, 1):
            if (index, half - 1, j) in hops:
                hops[index, half - 1, j].wait_recv()
                total = total + incoming[index, half - 1, chunk, :].astype(jnp.float32)
        out_ref[chunk, :] = total.astype(jnp.bfloat16)
    for copy in list(shares.values()) + list(hops.values()):
        copy.wait_send()


def sum_and_scatter(terms, residual):
    chips, heads = lax.axis_size("ctx") // CORES, lax.axis_size("head")
    rows, width = residual.shape
    half = chips * heads // 2
    parts = len(row_chunks(rows))
    return pl.pallas_call(
        functools.partial(sum_kernel, chips, heads),
        out_shape=jax.ShapeDtypeStruct((rows, width), jnp.bfloat16),
        in_specs=[full_vmem()] * 2,
        out_specs=full_vmem(),
        scratch_shapes=[
            pltpu.VMEM((2 * half, rows, width), jnp.bfloat16),
            pltpu.VMEM((2, half, rows, width), jnp.bfloat16),
            pltpu.VMEM((2, half, rows, width), jnp.bfloat16),
            pltpu.SemaphoreType.DMA((2 * half,)),
            pltpu.SemaphoreType.DMA((2 * half,)),
            pltpu.SemaphoreType.DMA((2, half, parts)),
            pltpu.SemaphoreType.DMA((2, half, parts)),
        ],
        compiler_params=pltpu.CompilerParams(collective_id=2, has_side_effects=True),
        name="sum_and_scatter",
    )(terms, residual)


def expert_activation(token_rows, w_gate_up):
    gate_pre = jnp.dot(token_rows, w_gate_up[0, 0], preferred_element_type=jnp.float32)
    up_pre = jnp.dot(token_rows, w_gate_up[0, 1], preferred_element_type=jnp.float32)
    return (gate_pre * jax.nn.sigmoid(1.702 * gate_pre) * (up_pre + 1.0)).astype(jnp.bfloat16)


def body(
    queries,
    keys,
    values,
    sinks,
    segments,
    hidden_in,
    routes,
    w_out,
    norm_gain,
    router,
    w_gate_up,
    w_down,
):
    n_ctx = lax.axis_size("ctx")
    n_head = lax.axis_size("head")
    tok_count = queries.shape[0]
    top_count = routes.shape[1]
    kv_groups = keys.shape[1] // HEAD_SIZE
    group_share = queries.shape[1] // (kv_groups * HEAD_SIZE)
    q_start = lax.axis_index("ctx") * tok_count
    tok_pos = q_start + jnp.arange(tok_count, dtype=jnp.int32)
    tok_seg = lax.dynamic_slice_in_dim(segments, q_start, tok_count, 0)
    query_grid = queries.reshape(tok_count, kv_groups, group_share, HEAD_SIZE)
    sink_grid = sinks.reshape(kv_groups, group_share, 1) * jnp.ones((1, 1, tok_count), jnp.float32)
    initial = (
        sink_grid,
        jnp.ones_like(sink_grid),
        jnp.zeros((kv_groups, group_share, tok_count, HEAD_SIZE), jnp.float32),
    )
    all_keys, all_values = gather_keys(keys, values)
    running_max, running_sum, weighted = fold_step(
        initial,
        (all_keys, all_values),
        query_grid,
        tok_pos,
        tok_seg,
        segments,
    )
    attended = (
        (weighted / running_sum[..., None])
        .transpose(2, 0, 1, 3)
        .reshape(tok_count, -1)
        .astype(jnp.bfloat16)
    )
    own_rows = tok_count // n_head
    row_start = lax.axis_index("head") * own_rows
    capacity = max(2, min(tok_count // n_head, 3 * tok_count * top_count // (2 * n_head * n_ctx)))
    partial_sums = jnp.dot(attended, w_out, preferred_element_type=jnp.float32).astype(jnp.bfloat16)
    own_hidden = lax.dynamic_slice_in_dim(hidden_in, row_start, own_rows, 0)
    own_routes = lax.dynamic_slice_in_dim(routes, row_start, own_rows, 0)
    residual, gathered = norm_and_gather(partial_sums, own_hidden, norm_gain, router, own_routes)
    width, experts = router.shape
    expert = lax.axis_index("ctx")
    blocks = n_ctx * n_head
    normed_all = gathered[:, :, :width]
    lanes = jnp.arange(2 * experts, dtype=jnp.int32)
    gate = jnp.sum(
        jnp.where(
            (lanes == expert) | (lanes == expert + experts),
            gathered[:, :, width : width + 2 * experts].astype(jnp.float32),
            0.0,
        ),
        axis=-1,
    )
    chosen = gate > 0.0
    rank = jnp.cumsum(chosen.astype(jnp.int32), axis=1) - 1
    place = (
        (rank[:, None, :] == jnp.arange(capacity, dtype=jnp.int32)[None, :, None])
        & chosen[:, None, :]
    )
    token_rows = jnp.einsum(
        "bcr,brd->bcd",
        place.astype(jnp.bfloat16),
        normed_all,
        preferred_element_type=jnp.float32,
    ).astype(jnp.bfloat16)
    row_gate = jnp.sum(jnp.where(place, gate[:, None, :], 0.0), axis=2).reshape(-1, 1)
    activation = expert_activation(token_rows.reshape(blocks * capacity, -1), w_gate_up)
    pieces = jnp.dot(activation, w_down[0], preferred_element_type=jnp.float32)
    gated = (pieces * row_gate).astype(jnp.bfloat16).reshape(blocks, capacity, -1)
    spread = jnp.einsum(
        "bcr,bcd->brd", place.astype(jnp.bfloat16), gated, preferred_element_type=jnp.float32
    ).astype(jnp.bfloat16)
    return sum_and_scatter(spread, residual)


def solution(mesh):
    placed = (
        P(("group", "ctx"), "head"),
        P(("group", "ctx"), "head"),
        P(("group", "ctx"), "head"),
        P("head"),
        P("group"),
        P(("group", "ctx"), None),
        P(("group", "ctx"), None),
        P("head", None),
        P(),
        P(),
        P("ctx", None, None, "head"),
        P("ctx", "head", None),
    )
    return jax.shard_map(
        body,
        mesh=mesh,
        in_specs=placed,
        out_specs=P(("group", "ctx", "head"), None),
        check_vma=False,
    )
```

```python
import functools

import jax
import jax.numpy as jnp
from jax import lax
from jax.experimental import pallas as pl
from jax.experimental.pallas import tpu as pltpu
from jax.sharding import PartitionSpec as P

HEAD_SIZE = 64


masked_value = -1e30


def fold_step(state_in, pieces, query_grid, tok_pos, tok_seg, segments):
    running_max, running_sum, weighted = state_in
    key_piece, value_piece = pieces
    row_count = key_piece.shape[0]
    kv_groups = query_grid.shape[1]
    key_grid = key_piece.reshape(row_count, kv_groups, -1)
    value_grid = value_piece.reshape(row_count, kv_groups, -1)
    scores = jnp.einsum(
        "tcgd,ncd->cgtn", query_grid, key_grid, preferred_element_type=jnp.float32
    ) * HEAD_SIZE ** (-0.5)
    key_pos = jnp.arange(row_count, dtype=jnp.int32)
    visible = (key_pos[None, :] <= tok_pos[:, None]) & (segments[None, :] == tok_seg[:, None])
    scores = jnp.where(visible, scores, masked_value)
    new_max = jnp.maximum(running_max, jnp.max(scores, axis=-1))
    weights = jnp.where(visible, jnp.exp(scores - new_max[..., None]), 0.0)
    rescale = jnp.exp(running_max - new_max)
    running_sum = running_sum * rescale + jnp.sum(weights, axis=-1)
    weighted = weighted * rescale[..., None] + jnp.einsum(
        "cgtn,ncd->cgtd",
        weights.astype(jnp.bfloat16),
        value_grid,
        preferred_element_type=jnp.float32,
    )
    return (new_max, running_sum, weighted)


MESH = pl.DeviceIdType.MESH
LANES = 128
CORES = 2


def full_vmem():
    return pl.BlockSpec(memory_space=pltpu.VMEM)


class Ring:
    def __init__(self, chips, heads):
        self.chips, self.heads, self.count = chips, heads, chips * heads
        ctx = lax.axis_index("ctx")
        self.head = lax.axis_index("head")
        self.core = lax.rem(ctx, CORES)
        z = lax.div(ctx, CORES)
        self.place = self.head * chips + z + lax.rem(self.head, 2) * (chips - 1 - 2 * z)
        self.partner = {"ctx": z * CORES + 1 - self.core, "head": self.head}

    def at(self, offset):
        spot = lax.rem(self.place + offset + self.count, self.count)
        head = lax.div(spot, self.chips)
        step = lax.rem(spot, self.chips)
        return head, step + lax.rem(head, 2) * (self.chips - 1 - 2 * step)

    def block(self, offset, core):
        head, z = self.at(offset)
        return (z * CORES + core) * self.heads + head

    def device(self, offset):
        head, z = self.at(offset)
        return {"ctx": z * CORES + self.core, "head": head}


def remote(src, dst, send_sem, recv_sem, device):
    return pltpu.make_async_remote_copy(
        src_ref=src, dst_ref=dst, send_sem=send_sem, recv_sem=recv_sem, device_id=device, device_id_type=MESH
    )


def greet(devices):
    barrier = pltpu.get_barrier_semaphore()
    for device in devices:
        pl.semaphore_signal(barrier, inc=1, device_id=device, device_id_type=MESH)
    pl.semaphore_wait(barrier, len(devices))


def row_chunks(rows):
    if rows % 32 == 0:
        return [pl.ds(0, rows // 2), pl.ds(rows // 2, rows // 2)]
    return [pl.ds(0, rows)]


def line_kernel(chips, key_ref, value_ref, all_keys, all_values, line_send, line_recv, pair_send, pair_recv, own_sem):
    ctx = lax.axis_index("ctx")
    z, core = lax.div(ctx, CORES), lax.rem(ctx, CORES)
    ins, outs = (key_ref, value_ref), (all_keys, all_values)
    partner = {"ctx": z * CORES + 1 - core}
    ways = ((0, 1), (1, -1))

    def inside(spot):
        return (spot >= 0) & (spot < chips)

    barrier = pltpu.get_barrier_semaphore()
    pl.semaphore_signal(barrier, inc=1, device_id=partner, device_id_type=MESH)
    for _, way in ways:

        @pl.when(inside(z + way))
        def _():
            pl.semaphore_signal(
                barrier, inc=1, device_id={"ctx": (z + way) * CORES + core}, device_id_type=MESH
            )

    peers = 1 + sum(jnp.where(inside(z + way), 1, 0) for _, way in ways)
    pl.semaphore_wait(barrier, peers)

    def hop(index, way, step, part):
        block = (z - way * step) * CORES + core
        source = ins[part] if step == 0 else outs[part].at[block]
        return remote(
            source,
            outs[part].at[block],
            line_send.at[index, step, part],
            line_recv.at[index, step, part],
            {"ctx": (z + way) * CORES + core},
        )

    def share(slot, block, part):
        source = ins[part] if slot == 0 else outs[part].at[block]
        return remote(source, outs[part].at[block], pair_send.at[slot, part], pair_recv.at[slot, part], partner)

    def keep(part):
        return pltpu.make_async_copy(ins[part], outs[part].at[ctx], own_sem.at[part])

    for part in (0, 1):
        for index, way in ways:

            @pl.when(inside(z + way))
            def _():
                hop(index, way, 0, part).start()

    for part in (0, 1):
        share(0, ctx, part).start()
        keep(part).start()
    for step in range(1, chips):
        for part in (0, 1):
            for index, way in ways:

                @pl.when(inside(z - way * step))
                def _():
                    hop(index, way, step - 1, part).wait_recv()
                    if step < chips - 1:

                        @pl.when(inside(z + way))
                        def _():
                            hop(index, way, step, part).start()

                    share(index * (chips - 1) + step, (z - way * step) * CORES + core, part).start()

    for part in (0, 1):
        keep(part).wait()
        share(0, ctx, part).wait()
        for index, way in ways:
            for step in range(chips):
                if step < chips - 1:

                    @pl.when(inside(z + way) & inside(z - way * step))
                    def _():
                        hop(index, way, step, part).wait_send()

                if step > 0:

                    @pl.when(inside(z - way * step))
                    def _():
                        share(index * (chips - 1) + step, (z - way * step) * CORES + core, part).wait()


def gather_keys(keys, values):
    n_ctx = lax.axis_size("ctx")
    chips = n_ctx // CORES
    shape = jax.ShapeDtypeStruct((n_ctx,) + keys.shape, keys.dtype)
    slots = 2 * (chips - 1) + 1
    gathered = pl.pallas_call(
        functools.partial(line_kernel, chips),
        out_shape=(shape, shape),
        in_specs=[full_vmem()] * 2,
        out_specs=(full_vmem(),) * 2,
        scratch_shapes=[
            pltpu.SemaphoreType.DMA((2, chips, 2)),
            pltpu.SemaphoreType.DMA((2, chips, 2)),
            pltpu.SemaphoreType.DMA((slots, 2)),
            pltpu.SemaphoreType.DMA((slots, 2)),
            pltpu.SemaphoreType.DMA((2,)),
        ],
        compiler_params=pltpu.CompilerParams(collective_id=0, has_side_effects=True),
        name="gather_keys",
    )(keys, values)
    return [array.reshape(-1, array.shape[-1]) for array in gathered]


def norm_kernel(
    chips, heads, experts, part_ref, hidden_ref, gain_ref, router_ref, route_ref, residual_ref, all_ref,
    slots, head_send, head_recv, ring_send, ring_recv, pair_send, pair_recv,
):
    ring = Ring(chips, heads)
    count, half = ring.count, ring.count // 2
    rows, width = hidden_ref.shape
    ctx, head = lax.axis_index("ctx"), ring.head
    others = [{"ctx": ctx, "head": lax.rem(head + turn, heads)} for turn in range(1, heads)]
    greet([ring.device(1), ring.device(-1), ring.partner] + others)

    sends = []
    for turn, device in enumerate(others):
        target = pl.ds(pl.multiple_of(device["head"] * rows, rows), rows)
        copy = remote(part_ref.at[target], slots.at[turn], head_send.at[turn], head_recv.at[turn], device)
        copy.start()
        sends.append(copy)
    own = pl.ds(pl.multiple_of(head * rows, rows), rows)
    total = hidden_ref[...].astype(jnp.float32) + part_ref[own, :].astype(jnp.float32)
    for turn, copy in enumerate(sends):
        copy.wait_recv()
        total = total + slots[turn].astype(jnp.float32)
    residual = total.astype(jnp.bfloat16)
    residual_ref[...] = residual
    wide = residual.astype(jnp.float32)
    scale = lax.rsqrt(jnp.mean(wide * wide, axis=-1, keepdims=True) + 1e-05)
    normed = (wide * scale * gain_ref[...]).astype(jnp.bfloat16)

    logits = lax.dot_general(
        normed, router_ref[...], (((1,), (1,)), ((), ())), preferred_element_type=jnp.float32
    )
    start = width % LANES
    lane = lax.broadcasted_iota(jnp.int32, logits.shape, 1) - start
    first = (lane >= 0) & (lane < experts)
    present = jnp.zeros(logits.shape, jnp.bool_)
    for k in range(route_ref.shape[1]):
        route = route_ref[:, k : k + 1]
        present = present | (lane == route) | (lane - experts == route)
    top = jnp.max(jnp.where(present, logits, -jnp.inf), axis=-1, keepdims=True)
    powers = jnp.where(present, jnp.exp(jnp.where(present, logits - top, 0.0)), 0.0)
    gates = powers / jnp.sum(jnp.where(first, powers, 0.0), axis=-1, keepdims=True)
    coarse = gates.astype(jnp.bfloat16)
    rest = gates - coarse.astype(jnp.float32)
    mine = ring.block(0, ring.core)
    all_ref[mine, :, width - start :] = jnp.where(first, coarse.astype(jnp.float32), rest).astype(jnp.bfloat16)
    all_ref[mine, :, :width] = normed

    chunks = row_chunks(rows)
    hops, shares = {}, []

    def share(slot, block, j):
        view = all_ref.at[block, chunks[j]]
        copy = remote(view, view, pair_send.at[slot, j], pair_recv.at[slot, j], ring.partner)
        copy.start()
        shares.append(copy)

    for step in range(half + 1):
        for j in range(len(chunks)):
            for index, way in ((0, 1), (1, -1)):
                block = ring.block(-way * step, ring.core)
                if step > 0 and (index, step - 1, j) in hops:
                    hops[index, step - 1, j].wait_recv()
                if step < half - 1 or (step == half - 1 and (j == 0) == (index == 0)):
                    view = all_ref.at[block, chunks[j]]
                    hops[index, step, j] = remote(
                        view, view, ring_send.at[index, step, j], ring_recv.at[index, step, j], ring.device(way)
                    )
                    hops[index, step, j].start()
                if step == 0 and index == 0:
                    share(0, block, j)
                elif step > 0 and (index, step - 1, j) in hops:
                    share(index * half + step, block, j)
    for copy in sends + list(hops.values()):
        copy.wait_send()
    for copy in shares:
        copy.wait()


def norm_and_gather(partial_sums, own_hidden, norm_gain, router, own_routes):
    chips, heads = lax.axis_size("ctx") // CORES, lax.axis_size("head")
    rows, width = own_hidden.shape
    experts = router.shape[1]
    start = width % LANES
    padded = width - start + LANES
    half = chips * heads // 2
    parts = len(row_chunks(rows))
    turned = router.T
    lanes = jnp.concatenate(
        [
            jnp.zeros((start, width), router.dtype),
            turned,
            turned,
            jnp.zeros((LANES - start - 2 * experts, width), router.dtype),
        ],
        axis=0,
    )
    return pl.pallas_call(
        functools.partial(norm_kernel, chips, heads, experts),
        out_shape=(
            jax.ShapeDtypeStruct((rows, width), jnp.bfloat16),
            jax.ShapeDtypeStruct((chips * heads * CORES, rows, padded), jnp.bfloat16),
        ),
        in_specs=[full_vmem()] * 5,
        out_specs=(full_vmem(),) * 2,
        scratch_shapes=[
            pltpu.VMEM((heads - 1, rows, width), jnp.bfloat16),
            pltpu.SemaphoreType.DMA((heads - 1,)),
            pltpu.SemaphoreType.DMA((heads - 1,)),
            pltpu.SemaphoreType.DMA((2, half, parts)),
            pltpu.SemaphoreType.DMA((2, half, parts)),
            pltpu.SemaphoreType.DMA((2 * half + 1, parts)),
            pltpu.SemaphoreType.DMA((2 * half + 1, parts)),
        ],
        compiler_params=pltpu.CompilerParams(collective_id=1, has_side_effects=True),
        name="norm_and_gather",
    )(partial_sums, own_hidden, norm_gain.reshape(1, -1), lanes, own_routes)


def row_placement(tail, expert, experts, start, capacity):
    rows = tail.shape[0]
    lane = lax.broadcasted_iota(jnp.int32, (LANES, tail.shape[1]), 1) - start
    pick = ((lane == expert) | (lane == expert + experts)).astype(jnp.float32).astype(jnp.bfloat16)
    spot = lax.broadcasted_iota(jnp.int32, (rows, rows), 0)
    other = lax.broadcasted_iota(jnp.int32, (rows, rows), 1)
    turned = (((1,), (1,)), ((), ()))
    across = lax.dot_general(pick, tail, turned, preferred_element_type=jnp.float32)
    before = (spot < other).astype(jnp.float32).astype(jnp.bfloat16)
    named = (across > 0.0).astype(jnp.float32)
    rank = jnp.dot(named.astype(jnp.bfloat16), before, preferred_element_type=jnp.float32)
    slot = lax.broadcasted_iota(jnp.int32, (capacity, rows), 0)
    match = (rank[:1] == slot.astype(jnp.float32)) & (named[:1] > 0.0)
    gate = jnp.sum(jnp.where(match, across[:1], 0.0), axis=1, keepdims=True)
    down = lax.dot_general(tail, pick, turned, preferred_element_type=jnp.float32)
    named_down = (down > 0.0).astype(jnp.float32)
    after = (spot > other).astype(jnp.float32).astype(jnp.bfloat16)
    rank_down = jnp.dot(after, named_down.astype(jnp.bfloat16), preferred_element_type=jnp.float32)
    slot_down = lax.broadcasted_iota(jnp.int32, (rows, capacity), 1)
    match_down = (rank_down[:, :1] == slot_down.astype(jnp.float32)) & (named_down[:, :1] > 0.0)
    return (
        match.astype(jnp.float32).astype(jnp.bfloat16),
        match_down.astype(jnp.float32).astype(jnp.bfloat16),
        gate,
    )


def expert_kernel(
    chips, heads, experts, capacity, tile, group_size, all_ref, residual_ref, up_hbm, down_hbm, out_ref,
    up_ref, down_ref, rows_ref, total_ref, gate_ref, back_ref, term_ref, got, outgoing, incoming,
    weight_sem, pair_send, pair_recv, ring_send, ring_recv,
):
    ring = Ring(chips, heads)
    half = ring.count // 2
    rows, width = residual_ref.shape
    start = width % LANES
    chunks = row_chunks(rows)
    expert = lax.axis_index("ctx")
    tiles = down_ref.shape[0] // tile

    def loads(t):
        span = pl.ds(pl.multiple_of(t * tile, 8), tile)
        return [
            pltpu.make_async_copy(up_hbm.at[0, span], up_ref.at[0, span], weight_sem.at[0, t]),
            pltpu.make_async_copy(up_hbm.at[1, span], up_ref.at[1, span], weight_sem.at[1, t]),
            pltpu.make_async_copy(down_hbm.at[span], down_ref.at[span], weight_sem.at[2, t]),
        ]

    for t in range(tiles):
        for copy in loads(t):
            copy.start()
    greet([ring.device(1), ring.device(-1), ring.partner])

    order = [half]
    for distance in range(half - 1, 0, -1):
        order += [distance, -distance]
    order.append(0)
    turned = (((1,), (1,)), ((), ()))

    def block_of(index):
        slot = lax.div(index, CORES)
        distance = half - lax.div(slot + 1, 2)
        sign = jnp.where(lax.rem(slot, 2) == 1, 1, -1)
        return ring.block(sign * distance, lax.rem(index, CORES))

    def compute(first, wait):
        def collect(i, carry):
            block = block_of(first + i)
            tail = all_ref[block, :, width - start :]
            place, back, gate = row_placement(tail, expert, experts, start, capacity)
            span = pl.ds(pl.multiple_of(i * capacity, 16), capacity)
            picked = jnp.dot(place, all_ref[block, :, :width], preferred_element_type=jnp.float32)
            rows_ref[span, :] = picked.astype(jnp.bfloat16)
            gate_ref[span, :] = gate
            back_ref[i] = back
            return carry

        lax.fori_loop(0, group_size, collect, 0)

        def multiply(t, carry):
            if wait:
                for copy in loads(t):
                    copy.wait()
            span = pl.ds(pl.multiple_of(t * tile, 8), tile)
            x = rows_ref[...]
            a = lax.dot_general(x, up_ref[0, span, :], turned, preferred_element_type=jnp.float32)
            b = lax.dot_general(x, up_ref[1, span, :], turned, preferred_element_type=jnp.float32)
            act = (a * jax.nn.sigmoid(1.702 * a) * (b + 1.0)).astype(jnp.bfloat16)
            piece = jnp.dot(act, down_ref[span, :], preferred_element_type=jnp.float32)

            @pl.when(t == 0)
            def _():
                total_ref[...] = piece

            @pl.when(t > 0)
            def _():
                total_ref[...] = total_ref[...] + piece

            return carry

        lax.fori_loop(0, tiles, multiply, 0)

        def spread(i, carry):
            span = pl.ds(pl.multiple_of(i * capacity, 16), capacity)
            gated = (total_ref[span, :] * gate_ref[span, :]).astype(jnp.bfloat16)
            term = jnp.dot(back_ref[i], gated, preferred_element_type=jnp.float32)
            term_ref[block_of(first + i)] = term.astype(jnp.bfloat16)
            return carry

        lax.fori_loop(0, group_size, spread, 0)

    shares, arrived, hops = {}, set(), {}

    def share(slot):
        offset = order[slot]
        shares[offset] = remote(
            term_ref.at[ring.block(offset, 1 - ring.core)],
            got.at[slot],
            pair_send.at[slot],
            pair_recv.at[slot],
            ring.partner,
        )
        shares[offset].start()

    def pair(offset, chunk):
        if offset == -half:
            offset = half
        if offset not in arrived:
            shares[offset].wait_recv()
            arrived.add(offset)
        mine = term_ref[ring.block(offset, ring.core), chunk, :].astype(jnp.float32)
        return mine + got[order.index(offset), chunk, :].astype(jnp.float32)

    def ring_step(step):
        for j, chunk in enumerate(chunks):
            for index, way in ((0, 1), (1, -1)):
                if step == 0 and (j == 0) != (index == 0):
                    continue
                total = pair(way * (half - step), chunk)
                if (index, step - 1, j) in hops:
                    hops[index, step - 1, j].wait_recv()
                    total = total + incoming[index, step - 1, chunk, :].astype(jnp.float32)
                outgoing[index, step, chunk, :] = total.astype(jnp.bfloat16)
                hops[index, step, j] = remote(
                    outgoing.at[index, step, chunk],
                    incoming.at[index, step, chunk],
                    ring_send.at[index, step, j],
                    ring_recv.at[index, step, j],
                    ring.device(way),
                )
                hops[index, step, j].start()

    blocks, step = ring.count * CORES, 0
    for first in range(0, blocks, group_size):
        compute(first, first == 0)
        done = (first + group_size) // CORES
        for slot in range(first // CORES, done):
            share(slot)
        while step < half and 2 * step + 1 <= done:
            ring_step(step)
            step += 1
    for j, chunk in enumerate(chunks):
        total = pair(0, chunk) + residual_ref[chunk, :].astype(jnp.float32)
        for index in (0, 1):
            if (index, half - 1, j) in hops:
                hops[index, half - 1, j].wait_recv()
                total = total + incoming[index, half - 1, chunk, :].astype(jnp.float32)
        out_ref[chunk, :] = total.astype(jnp.bfloat16)
    for copy in list(shares.values()) + list(hops.values()):
        copy.wait_send()


def experts_and_sum(gathered, residual, w_gate_up, w_down, experts, capacity):
    chips, heads = lax.axis_size("ctx") // CORES, lax.axis_size("head")
    rows, width = residual.shape
    hidden = w_down.shape[1]
    half = chips * heads // 2
    blocks = gathered.shape[0]
    parts = len(row_chunks(rows))
    capacity = -(-capacity // 16) * 16
    tile = hidden // 3 if hidden % 48 == 0 else hidden
    group_size = blocks // 4
    bf16, dma = jnp.bfloat16, pltpu.SemaphoreType.DMA
    anywhere = pl.BlockSpec(memory_space=pl.ANY)
    return pl.pallas_call(
        functools.partial(expert_kernel, chips, heads, experts, capacity, tile, group_size),
        out_shape=jax.ShapeDtypeStruct((rows, width), bf16),
        in_specs=[full_vmem(), full_vmem(), anywhere, anywhere],
        out_specs=full_vmem(),
        scratch_shapes=[
            pltpu.VMEM((2, hidden, width), bf16),
            pltpu.VMEM((hidden, width), bf16),
            pltpu.VMEM((group_size * capacity, width), bf16),
            pltpu.VMEM((group_size * capacity, width), jnp.float32),
            pltpu.VMEM((group_size * capacity, 1), jnp.float32),
            pltpu.VMEM((group_size, rows, capacity), bf16),
            pltpu.VMEM((blocks, rows, width), bf16),
            pltpu.VMEM((2 * half, rows, width), bf16),
            pltpu.VMEM((2, half, rows, width), bf16),
            pltpu.VMEM((2, half, rows, width), bf16),
            dma((3, hidden // tile)),
            dma((2 * half,)),
            dma((2 * half,)),
            dma((2, half, parts)),
            dma((2, half, parts)),
        ],
        compiler_params=pltpu.CompilerParams(
            collective_id=2, has_side_effects=True, vmem_limit_bytes=60 * 1024 * 1024
        ),
        name="experts_and_sum",
    )(gathered, residual, jnp.swapaxes(w_gate_up[0], 1, 2), w_down[0])


def body(
    queries,
    keys,
    values,
    sinks,
    segments,
    hidden_in,
    routes,
    w_out,
    norm_gain,
    router,
    w_gate_up,
    w_down,
):
    n_ctx = lax.axis_size("ctx")
    n_head = lax.axis_size("head")
    tok_count = queries.shape[0]
    top_count = routes.shape[1]
    kv_groups = keys.shape[1] // HEAD_SIZE
    group_share = queries.shape[1] // (kv_groups * HEAD_SIZE)
    q_start = lax.axis_index("ctx") * tok_count
    tok_pos = q_start + jnp.arange(tok_count, dtype=jnp.int32)
    tok_seg = lax.dynamic_slice_in_dim(segments, q_start, tok_count, 0)
    query_grid = queries.reshape(tok_count, kv_groups, group_share, HEAD_SIZE)
    sink_grid = sinks.reshape(kv_groups, group_share, 1) * jnp.ones((1, 1, tok_count), jnp.float32)
    initial = (
        sink_grid,
        jnp.ones_like(sink_grid),
        jnp.zeros((kv_groups, group_share, tok_count, HEAD_SIZE), jnp.float32),
    )
    all_keys, all_values = gather_keys(keys, values)
    running_max, running_sum, weighted = fold_step(
        initial,
        (all_keys, all_values),
        query_grid,
        tok_pos,
        tok_seg,
        segments,
    )
    attended = (
        (weighted / running_sum[..., None])
        .transpose(2, 0, 1, 3)
        .reshape(tok_count, -1)
        .astype(jnp.bfloat16)
    )
    own_rows = tok_count // n_head
    row_start = lax.axis_index("head") * own_rows
    capacity = max(2, min(tok_count // n_head, 3 * tok_count * top_count // (2 * n_head * n_ctx)))
    partial_sums = jnp.dot(attended, w_out, preferred_element_type=jnp.float32).astype(jnp.bfloat16)
    own_hidden = lax.dynamic_slice_in_dim(hidden_in, row_start, own_rows, 0)
    own_routes = lax.dynamic_slice_in_dim(routes, row_start, own_rows, 0)
    residual, gathered = norm_and_gather(partial_sums, own_hidden, norm_gain, router, own_routes)
    return experts_and_sum(gathered, residual, w_gate_up, w_down, router.shape[1], capacity)


def solution(mesh):
    placed = (
        P(("group", "ctx"), "head"),
        P(("group", "ctx"), "head"),
        P(("group", "ctx"), "head"),
        P("head"),
        P("group"),
        P(("group", "ctx"), None),
        P(("group", "ctx"), None),
        P("head", None),
        P(),
        P(),
        P("ctx", None, None, "head"),
        P("ctx", "head", None),
    )
    return jax.shard_map(
        body,
        mesh=mesh,
        in_specs=placed,
        out_specs=P(("group", "ctx", "head"), None),
        check_vma=False,
    )
```

```python
import functools

import jax
import jax.numpy as jnp
from jax import lax
from jax.experimental import pallas as pl
from jax.experimental.pallas import tpu as pltpu
from jax.sharding import PartitionSpec as P

HEAD_SIZE = 64


masked_value = -1e30


def attend_kernel(
    query_ref, key_ref, value_ref, sink_ref, place_ref, segment_ref, own_segment_ref, out_ref
):
    rows = query_ref.shape[0]
    kv_groups = key_ref.shape[1] // HEAD_SIZE
    share = query_ref.shape[1] // key_ref.shape[1]
    spot = lax.broadcasted_iota(jnp.int32, (rows, key_ref.shape[0]), 1)
    visible = (spot <= place_ref[...]) & (segment_ref[...] == own_segment_ref[...])
    hidden_bias = jnp.where(visible, 0.0, masked_value)
    for group in range(kv_groups):
        span = slice(group * HEAD_SIZE, (group + 1) * HEAD_SIZE)
        group_keys = key_ref[:, span]
        group_values = value_ref[:, span]
        for pair in range(share // 2):
            both = []
            for member in range(2):
                head = group * share + pair * 2 + member
                query = query_ref[:, head * HEAD_SIZE : (head + 1) * HEAD_SIZE]
                scores = lax.dot_general(
                    query, group_keys, (((1,), (1,)), ((), ())), preferred_element_type=jnp.float32
                )
                scores = scores * HEAD_SIZE ** (-0.5) + hidden_bias
                sink = sink_ref[:, head : head + 1]
                top = jnp.maximum(jnp.max(scores, axis=-1, keepdims=True), sink)
                weights = jnp.exp(scores - top)
                total = jnp.sum(weights, axis=-1, keepdims=True) + jnp.exp(sink - top)
                mixed = jnp.dot(weights.astype(jnp.bfloat16), group_values, preferred_element_type=jnp.float32)
                both.append((mixed / total).astype(jnp.bfloat16))
            first = (group * share + pair * 2) * HEAD_SIZE
            out_ref[:, first : first + 2 * HEAD_SIZE] = jnp.concatenate(both, axis=1)


def attend(queries, all_keys, all_values, sinks, tok_pos, tok_seg, segments):
    return pl.pallas_call(
        attend_kernel,
        out_shape=jax.ShapeDtypeStruct(queries.shape, jnp.bfloat16),
        in_specs=[full_vmem()] * 7,
        out_specs=full_vmem(),
        name="attend",
    )(
        queries,
        all_keys,
        all_values,
        sinks.reshape(1, -1),
        tok_pos.reshape(-1, 1),
        segments.reshape(1, -1),
        tok_seg.reshape(-1, 1),
    )


MESH = pl.DeviceIdType.MESH
LANES = 128
CORES = 2


def full_vmem():
    return pl.BlockSpec(memory_space=pltpu.VMEM)


class Ring:
    def __init__(self, chips, heads):
        self.chips, self.heads, self.count = chips, heads, chips * heads
        ctx = lax.axis_index("ctx")
        self.head = lax.axis_index("head")
        self.core = lax.rem(ctx, CORES)
        z = lax.div(ctx, CORES)
        self.place = self.head * chips + z + lax.rem(self.head, 2) * (chips - 1 - 2 * z)
        self.partner = {"ctx": z * CORES + 1 - self.core, "head": self.head}

    def at(self, offset):
        spot = lax.rem(self.place + offset + self.count, self.count)
        head = lax.div(spot, self.chips)
        step = lax.rem(spot, self.chips)
        return head, step + lax.rem(head, 2) * (self.chips - 1 - 2 * step)

    def block(self, offset, core):
        head, z = self.at(offset)
        return (z * CORES + core) * self.heads + head

    def device(self, offset):
        head, z = self.at(offset)
        return {"ctx": z * CORES + self.core, "head": head}


def remote(src, dst, send_sem, recv_sem, device):
    return pltpu.make_async_remote_copy(
        src_ref=src, dst_ref=dst, send_sem=send_sem, recv_sem=recv_sem, device_id=device, device_id_type=MESH
    )


def greet(devices):
    barrier = pltpu.get_barrier_semaphore()
    for device in devices:
        pl.semaphore_signal(barrier, inc=1, device_id=device, device_id_type=MESH)
    pl.semaphore_wait(barrier, len(devices))


def row_chunks(rows):
    if rows % 32 == 0:
        return [pl.ds(0, rows // 2), pl.ds(rows // 2, rows // 2)]
    return [pl.ds(0, rows)]


def line_kernel(chips, key_ref, value_ref, all_keys, all_values, line_send, line_recv, pair_send, pair_recv, own_sem):
    ctx = lax.axis_index("ctx")
    z, core = lax.div(ctx, CORES), lax.rem(ctx, CORES)
    ins, outs = (key_ref, value_ref), (all_keys, all_values)
    partner = {"ctx": z * CORES + 1 - core}
    ways = ((0, 1), (1, -1))

    def inside(spot):
        return (spot >= 0) & (spot < chips)

    barrier = pltpu.get_barrier_semaphore()
    pl.semaphore_signal(barrier, inc=1, device_id=partner, device_id_type=MESH)
    for _, way in ways:

        @pl.when(inside(z + way))
        def _():
            pl.semaphore_signal(
                barrier, inc=1, device_id={"ctx": (z + way) * CORES + core}, device_id_type=MESH
            )

    peers = 1 + sum(jnp.where(inside(z + way), 1, 0) for _, way in ways)
    pl.semaphore_wait(barrier, peers)

    def hop(index, way, step, part):
        block = (z - way * step) * CORES + core
        source = ins[part] if step == 0 else outs[part].at[block]
        return remote(
            source,
            outs[part].at[block],
            line_send.at[index, step, part],
            line_recv.at[index, step, part],
            {"ctx": (z + way) * CORES + core},
        )

    def share(slot, block, part):
        source = ins[part] if slot == 0 else outs[part].at[block]
        return remote(source, outs[part].at[block], pair_send.at[slot, part], pair_recv.at[slot, part], partner)

    def keep(part):
        return pltpu.make_async_copy(ins[part], outs[part].at[ctx], own_sem.at[part])

    for part in (0, 1):
        for index, way in ways:

            @pl.when(inside(z + way))
            def _():
                hop(index, way, 0, part).start()

    for part in (0, 1):
        share(0, ctx, part).start()
        keep(part).start()
    for step in range(1, chips):
        for part in (0, 1):
            for index, way in ways:

                @pl.when(inside(z - way * step))
                def _():
                    hop(index, way, step - 1, part).wait_recv()
                    if step < chips - 1:

                        @pl.when(inside(z + way))
                        def _():
                            hop(index, way, step, part).start()

                    share(index * (chips - 1) + step, (z - way * step) * CORES + core, part).start()

    for part in (0, 1):
        keep(part).wait()
        share(0, ctx, part).wait()
        for index, way in ways:
            for step in range(chips):
                if step < chips - 1:

                    @pl.when(inside(z + way) & inside(z - way * step))
                    def _():
                        hop(index, way, step, part).wait_send()

                if step > 0:

                    @pl.when(inside(z - way * step))
                    def _():
                        share(index * (chips - 1) + step, (z - way * step) * CORES + core, part).wait()


def gather_keys(keys, values):
    n_ctx = lax.axis_size("ctx")
    chips = n_ctx // CORES
    shape = jax.ShapeDtypeStruct((n_ctx,) + keys.shape, keys.dtype)
    slots = 2 * (chips - 1) + 1
    gathered = pl.pallas_call(
        functools.partial(line_kernel, chips),
        out_shape=(shape, shape),
        in_specs=[full_vmem()] * 2,
        out_specs=(full_vmem(),) * 2,
        scratch_shapes=[
            pltpu.SemaphoreType.DMA((2, chips, 2)),
            pltpu.SemaphoreType.DMA((2, chips, 2)),
            pltpu.SemaphoreType.DMA((slots, 2)),
            pltpu.SemaphoreType.DMA((slots, 2)),
            pltpu.SemaphoreType.DMA((2,)),
        ],
        compiler_params=pltpu.CompilerParams(collective_id=0, has_side_effects=True),
        name="gather_keys",
    )(keys, values)
    return [array.reshape(-1, array.shape[-1]) for array in gathered]


def norm_kernel(
    chips, heads, experts, part_ref, hidden_ref, gain_ref, router_ref, route_ref, residual_ref, all_ref,
    slots, head_send, head_recv, ring_send, ring_recv, pair_send, pair_recv,
):
    ring = Ring(chips, heads)
    count, half = ring.count, ring.count // 2
    rows, width = hidden_ref.shape
    ctx, head = lax.axis_index("ctx"), ring.head
    others = [{"ctx": ctx, "head": lax.rem(head + turn, heads)} for turn in range(1, heads)]
    greet([ring.device(1), ring.device(-1), ring.partner] + others)

    sends = []
    for turn, device in enumerate(others):
        target = pl.ds(pl.multiple_of(device["head"] * rows, rows), rows)
        copy = remote(part_ref.at[target], slots.at[turn], head_send.at[turn], head_recv.at[turn], device)
        copy.start()
        sends.append(copy)
    own = pl.ds(pl.multiple_of(head * rows, rows), rows)
    total = hidden_ref[...].astype(jnp.float32) + part_ref[own, :].astype(jnp.float32)
    for turn, copy in enumerate(sends):
        copy.wait_recv()
        total = total + slots[turn].astype(jnp.float32)
    residual = total.astype(jnp.bfloat16)
    residual_ref[...] = residual
    wide = residual.astype(jnp.float32)
    scale = lax.rsqrt(jnp.mean(wide * wide, axis=-1, keepdims=True) + 1e-05)
    normed = (wide * scale * gain_ref[...]).astype(jnp.bfloat16)

    logits = lax.dot_general(
        normed, router_ref[...], (((1,), (1,)), ((), ())), preferred_element_type=jnp.float32
    )
    start = width % LANES
    lane = lax.broadcasted_iota(jnp.int32, logits.shape, 1) - start
    first = (lane >= 0) & (lane < experts)
    present = jnp.zeros(logits.shape, jnp.bool_)
    for k in range(route_ref.shape[1]):
        route = route_ref[:, k : k + 1]
        present = present | (lane == route) | (lane - experts == route)
    top = jnp.max(jnp.where(present, logits, -jnp.inf), axis=-1, keepdims=True)
    powers = jnp.where(present, jnp.exp(jnp.where(present, logits - top, 0.0)), 0.0)
    gates = powers / jnp.sum(jnp.where(first, powers, 0.0), axis=-1, keepdims=True)
    coarse = gates.astype(jnp.bfloat16)
    rest = gates - coarse.astype(jnp.float32)
    mine = ring.block(0, ring.core)
    all_ref[mine, :, width - start :] = jnp.where(first, coarse.astype(jnp.float32), rest).astype(jnp.bfloat16)
    all_ref[mine, :, :width] = normed

    chunks = row_chunks(rows)
    hops, shares = {}, []

    def share(slot, block, j):
        view = all_ref.at[block, chunks[j]]
        copy = remote(view, view, pair_send.at[slot, j], pair_recv.at[slot, j], ring.partner)
        copy.start()
        shares.append(copy)

    for step in range(half + 1):
        for j in range(len(chunks)):
            for index, way in ((0, 1), (1, -1)):
                block = ring.block(-way * step, ring.core)
                if step > 0 and (index, step - 1, j) in hops:
                    hops[index, step - 1, j].wait_recv()
                if step < half - 1 or (step == half - 1 and (j == 0) == (index == 0)):
                    view = all_ref.at[block, chunks[j]]
                    hops[index, step, j] = remote(
                        view, view, ring_send.at[index, step, j], ring_recv.at[index, step, j], ring.device(way)
                    )
                    hops[index, step, j].start()
                if step == 0 and index == 0:
                    share(0, block, j)
                elif step > 0 and (index, step - 1, j) in hops:
                    share(index * half + step, block, j)
    for copy in sends + list(hops.values()):
        copy.wait_send()
    for copy in shares:
        copy.wait()


def norm_and_gather(partial_sums, own_hidden, norm_gain, router, own_routes):
    chips, heads = lax.axis_size("ctx") // CORES, lax.axis_size("head")
    rows, width = own_hidden.shape
    experts = router.shape[1]
    start = width % LANES
    padded = width - start + LANES
    half = chips * heads // 2
    parts = len(row_chunks(rows))
    turned = router.T
    lanes = jnp.concatenate(
        [
            jnp.zeros((start, width), router.dtype),
            turned,
            turned,
            jnp.zeros((LANES - start - 2 * experts, width), router.dtype),
        ],
        axis=0,
    )
    return pl.pallas_call(
        functools.partial(norm_kernel, chips, heads, experts),
        out_shape=(
            jax.ShapeDtypeStruct((rows, width), jnp.bfloat16),
            jax.ShapeDtypeStruct((chips * heads * CORES, rows, padded), jnp.bfloat16),
        ),
        in_specs=[full_vmem()] * 5,
        out_specs=(full_vmem(),) * 2,
        scratch_shapes=[
            pltpu.VMEM((heads - 1, rows, width), jnp.bfloat16),
            pltpu.SemaphoreType.DMA((heads - 1,)),
            pltpu.SemaphoreType.DMA((heads - 1,)),
            pltpu.SemaphoreType.DMA((2, half, parts)),
            pltpu.SemaphoreType.DMA((2, half, parts)),
            pltpu.SemaphoreType.DMA((2 * half + 1, parts)),
            pltpu.SemaphoreType.DMA((2 * half + 1, parts)),
        ],
        compiler_params=pltpu.CompilerParams(collective_id=1, has_side_effects=True),
        name="norm_and_gather",
    )(partial_sums, own_hidden, norm_gain.reshape(1, -1), lanes, own_routes)


def row_placement(tail, expert, experts, start, capacity):
    rows = tail.shape[0]
    lane = lax.broadcasted_iota(jnp.int32, (LANES, tail.shape[1]), 1) - start
    pick = ((lane == expert) | (lane == expert + experts)).astype(jnp.float32).astype(jnp.bfloat16)
    spot = lax.broadcasted_iota(jnp.int32, (rows, rows), 0)
    other = lax.broadcasted_iota(jnp.int32, (rows, rows), 1)
    turned = (((1,), (1,)), ((), ()))
    across = lax.dot_general(pick, tail, turned, preferred_element_type=jnp.float32)
    before = (spot < other).astype(jnp.float32).astype(jnp.bfloat16)
    named = (across > 0.0).astype(jnp.float32)
    rank = jnp.dot(named.astype(jnp.bfloat16), before, preferred_element_type=jnp.float32)
    slot = lax.broadcasted_iota(jnp.int32, (capacity, rows), 0)
    match = (rank[:1] == slot.astype(jnp.float32)) & (named[:1] > 0.0)
    gate = jnp.sum(jnp.where(match, across[:1], 0.0), axis=1, keepdims=True)
    down = lax.dot_general(tail, pick, turned, preferred_element_type=jnp.float32)
    named_down = (down > 0.0).astype(jnp.float32)
    after = (spot > other).astype(jnp.float32).astype(jnp.bfloat16)
    rank_down = jnp.dot(after, named_down.astype(jnp.bfloat16), preferred_element_type=jnp.float32)
    slot_down = lax.broadcasted_iota(jnp.int32, (rows, capacity), 1)
    match_down = (rank_down[:, :1] == slot_down.astype(jnp.float32)) & (named_down[:, :1] > 0.0)
    return (
        match.astype(jnp.float32).astype(jnp.bfloat16),
        match_down.astype(jnp.float32).astype(jnp.bfloat16),
        gate,
    )


def expert_kernel(
    chips, heads, experts, capacity, tile, group_size, all_ref, residual_ref, up_hbm, down_hbm, out_ref,
    up_ref, down_ref, rows_ref, total_ref, gate_ref, back_ref, term_ref, got, outgoing, incoming,
    weight_sem, pair_send, pair_recv, ring_send, ring_recv,
):
    ring = Ring(chips, heads)
    half = ring.count // 2
    rows, width = residual_ref.shape
    start = width % LANES
    chunks = row_chunks(rows)
    expert = lax.axis_index("ctx")
    tiles = down_ref.shape[0] // tile

    def loads(t):
        span = pl.ds(pl.multiple_of(t * tile, 8), tile)
        return [
            pltpu.make_async_copy(up_hbm.at[0, span], up_ref.at[0, span], weight_sem.at[0, t]),
            pltpu.make_async_copy(up_hbm.at[1, span], up_ref.at[1, span], weight_sem.at[1, t]),
            pltpu.make_async_copy(down_hbm.at[span], down_ref.at[span], weight_sem.at[2, t]),
        ]

    for t in range(tiles):
        for copy in loads(t):
            copy.start()
    greet([ring.device(1), ring.device(-1), ring.partner])

    order = [half]
    for distance in range(half - 1, 0, -1):
        order += [distance, -distance]
    order.append(0)
    turned = (((1,), (1,)), ((), ()))

    def block_of(index):
        slot = lax.div(index, CORES)
        distance = half - lax.div(slot + 1, 2)
        sign = jnp.where(lax.rem(slot, 2) == 1, 1, -1)
        return ring.block(sign * distance, lax.rem(index, CORES))

    def compute(first, wait):
        def collect(i, carry):
            block = block_of(first + i)
            tail = all_ref[block, :, width - start :]
            place, back, gate = row_placement(tail, expert, experts, start, capacity)
            span = pl.ds(pl.multiple_of(i * capacity, 16), capacity)
            picked = jnp.dot(place, all_ref[block, :, :width], preferred_element_type=jnp.float32)
            rows_ref[span, :] = picked.astype(jnp.bfloat16)
            gate_ref[span, :] = gate
            back_ref[i] = back
            return carry

        lax.fori_loop(0, group_size, collect, 0)

        def multiply(t, carry):
            if wait:
                for copy in loads(t):
                    copy.wait()
            span = pl.ds(pl.multiple_of(t * tile, 8), tile)
            x = rows_ref[...]
            a = lax.dot_general(x, up_ref[0, span, :], turned, preferred_element_type=jnp.float32)
            b = lax.dot_general(x, up_ref[1, span, :], turned, preferred_element_type=jnp.float32)
            act = (a * jax.nn.sigmoid(1.702 * a) * (b + 1.0)).astype(jnp.bfloat16)
            piece = jnp.dot(act, down_ref[span, :], preferred_element_type=jnp.float32)

            @pl.when(t == 0)
            def _():
                total_ref[...] = piece

            @pl.when(t > 0)
            def _():
                total_ref[...] = total_ref[...] + piece

            return carry

        lax.fori_loop(0, tiles, multiply, 0)

        def spread(i, carry):
            span = pl.ds(pl.multiple_of(i * capacity, 16), capacity)
            gated = (total_ref[span, :] * gate_ref[span, :]).astype(jnp.bfloat16)
            term = jnp.dot(back_ref[i], gated, preferred_element_type=jnp.float32)
            term_ref[block_of(first + i)] = term.astype(jnp.bfloat16)
            return carry

        lax.fori_loop(0, group_size, spread, 0)

    shares, arrived, hops = {}, set(), {}

    def share(slot):
        offset = order[slot]
        shares[offset] = remote(
            term_ref.at[ring.block(offset, 1 - ring.core)],
            got.at[slot],
            pair_send.at[slot],
            pair_recv.at[slot],
            ring.partner,
        )
        shares[offset].start()

    def pair(offset, chunk):
        if offset == -half:
            offset = half
        if offset not in arrived:
            shares[offset].wait_recv()
            arrived.add(offset)
        mine = term_ref[ring.block(offset, ring.core), chunk, :].astype(jnp.float32)
        return mine + got[order.index(offset), chunk, :].astype(jnp.float32)

    def ring_step(step):
        for j, chunk in enumerate(chunks):
            for index, way in ((0, 1), (1, -1)):
                if step == 0 and (j == 0) != (index == 0):
                    continue
                total = pair(way * (half - step), chunk)
                if (index, step - 1, j) in hops:
                    hops[index, step - 1, j].wait_recv()
                    total = total + incoming[index, step - 1, chunk, :].astype(jnp.float32)
                outgoing[index, step, chunk, :] = total.astype(jnp.bfloat16)
                hops[index, step, j] = remote(
                    outgoing.at[index, step, chunk],
                    incoming.at[index, step, chunk],
                    ring_send.at[index, step, j],
                    ring_recv.at[index, step, j],
                    ring.device(way),
                )
                hops[index, step, j].start()

    blocks, step = ring.count * CORES, 0
    for first in range(0, blocks, group_size):
        compute(first, first == 0)
        done = (first + group_size) // CORES
        for slot in range(first // CORES, done):
            share(slot)
        while step < half and 2 * step + 1 <= done:
            ring_step(step)
            step += 1
    for j, chunk in enumerate(chunks):
        total = pair(0, chunk) + residual_ref[chunk, :].astype(jnp.float32)
        for index in (0, 1):
            if (index, half - 1, j) in hops:
                hops[index, half - 1, j].wait_recv()
                total = total + incoming[index, half - 1, chunk, :].astype(jnp.float32)
        out_ref[chunk, :] = total.astype(jnp.bfloat16)
    for copy in list(shares.values()) + list(hops.values()):
        copy.wait_send()


def experts_and_sum(gathered, residual, w_gate_up, w_down, experts, capacity):
    chips, heads = lax.axis_size("ctx") // CORES, lax.axis_size("head")
    rows, width = residual.shape
    hidden = w_down.shape[1]
    half = chips * heads // 2
    blocks = gathered.shape[0]
    parts = len(row_chunks(rows))
    capacity = -(-capacity // 16) * 16
    tile = hidden // 3 if hidden % 48 == 0 else hidden
    group_size = blocks // 4
    bf16, dma = jnp.bfloat16, pltpu.SemaphoreType.DMA
    anywhere = pl.BlockSpec(memory_space=pl.ANY)
    return pl.pallas_call(
        functools.partial(expert_kernel, chips, heads, experts, capacity, tile, group_size),
        out_shape=jax.ShapeDtypeStruct((rows, width), bf16),
        in_specs=[full_vmem(), full_vmem(), anywhere, anywhere],
        out_specs=full_vmem(),
        scratch_shapes=[
            pltpu.VMEM((2, hidden, width), bf16),
            pltpu.VMEM((hidden, width), bf16),
            pltpu.VMEM((group_size * capacity, width), bf16),
            pltpu.VMEM((group_size * capacity, width), jnp.float32),
            pltpu.VMEM((group_size * capacity, 1), jnp.float32),
            pltpu.VMEM((group_size, rows, capacity), bf16),
            pltpu.VMEM((blocks, rows, width), bf16),
            pltpu.VMEM((2 * half, rows, width), bf16),
            pltpu.VMEM((2, half, rows, width), bf16),
            pltpu.VMEM((2, half, rows, width), bf16),
            dma((3, hidden // tile)),
            dma((2 * half,)),
            dma((2 * half,)),
            dma((2, half, parts)),
            dma((2, half, parts)),
        ],
        compiler_params=pltpu.CompilerParams(
            collective_id=2, has_side_effects=True, vmem_limit_bytes=60 * 1024 * 1024
        ),
        name="experts_and_sum",
    )(gathered, residual, jnp.swapaxes(w_gate_up[0], 1, 2), w_down[0])


def body(
    queries,
    keys,
    values,
    sinks,
    segments,
    hidden_in,
    routes,
    w_out,
    norm_gain,
    router,
    w_gate_up,
    w_down,
):
    n_ctx = lax.axis_size("ctx")
    n_head = lax.axis_size("head")
    tok_count = queries.shape[0]
    top_count = routes.shape[1]
    q_start = lax.axis_index("ctx") * tok_count
    tok_pos = q_start + jnp.arange(tok_count, dtype=jnp.int32)
    tok_seg = lax.dynamic_slice_in_dim(segments, q_start, tok_count, 0)
    all_keys, all_values = gather_keys(keys, values)
    attended = attend(queries, all_keys, all_values, sinks, tok_pos, tok_seg, segments)
    own_rows = tok_count // n_head
    row_start = lax.axis_index("head") * own_rows
    capacity = max(2, min(tok_count // n_head, 3 * tok_count * top_count // (2 * n_head * n_ctx)))
    partial_sums = jnp.dot(attended, w_out, preferred_element_type=jnp.float32).astype(jnp.bfloat16)
    own_hidden = lax.dynamic_slice_in_dim(hidden_in, row_start, own_rows, 0)
    own_routes = lax.dynamic_slice_in_dim(routes, row_start, own_rows, 0)
    residual, gathered = norm_and_gather(partial_sums, own_hidden, norm_gain, router, own_routes)
    return experts_and_sum(gathered, residual, w_gate_up, w_down, router.shape[1], capacity)


def solution(mesh):
    placed = (
        P(("group", "ctx"), "head"),
        P(("group", "ctx"), "head"),
        P(("group", "ctx"), "head"),
        P("head"),
        P("group"),
        P(("group", "ctx"), None),
        P(("group", "ctx"), None),
        P("head", None),
        P(),
        P(),
        P("ctx", None, None, "head"),
        P("ctx", "head", None),
    )
    return jax.shard_map(
        body,
        mesh=mesh,
        in_specs=placed,
        out_specs=P(("group", "ctx", "head"), None),
        check_vma=False,
    )
```
